256 devices in a mesh: section: 4 (over y), expert: 64 (over z, x, core).
Axes of the slice: x: 4, y: 4, z: 8, core: 2. Of those that a mesh axis runs over, the one named last changes fastest.
Arguments:
- inputs: bfloat16 [4, 192, 3072], P(None, 'expert'), may hold values from -6 to 6
- routes: int32 [4, 4, 192, 2], P('section'), may hold values from 0 to 3, all different within a row; in each aligned block of 3 rows (0 to 2, 3 to 5, ..., all dimensions but the last counted through in order) at most 2 rows name the same one
- norm_gain: float32 [4, 3072], P('section'), may hold values from 0.5 to 1.5
- router: bfloat16 [4, 3072, 4], P('section'), may hold values from -0.109375 to 0.109375
- w_gate: bfloat16 [4, 3072, 32768], P('section', None, 'expert'), may hold values from -0.109375 to 0.109375
- w_up: bfloat16 [4, 3072, 32768], P('section', None, 'expert'), may hold values from -0.109375 to 0.109375
- w_down: bfloat16 [4, 32768, 3072], P('section', 'expert'), may hold values from -0.0625 to 0.0625
Outputs:
- layer_outputs: bfloat16 [4, 4, 192, 3072], P('section', None, 'expert')
The draws below stay inside these ranges and needn't reach their ends.
Inputs may be any that keep to these rules, and one draw needn't show every extreme that they name: `routes`: for each section and micro-batch, the 3 requests of each aligned block name no expert more than 2 times, and a request's two experts differ.
All inputs are finite; a program needn't handle non-finite values.
Results may differ from the reference program's by a relative error of at most 0.017.
Values may be sent and summed in bfloat16 or wider, within the bound.
No kernel may reach another device: no remote copies, remote signals or barrier semaphores. Data moves between devices by JAX's collectives and lax.ppermute only.
A program may use at most 64 MiB of HBM per device.

```python
import math
from functools import partial
import jax
import jax.numpy as jnp
import numpy as np
from jax import lax

D = 3072
E = 4
FF = 8192
MICRO = 4
TOK_MB = 3
MOST = 2
FF_DEV = 512
TOKENS = 192
N_SECTION = 4
N_EXPERT = 64


def shard_levels(stream_key, dims, shards, least, high):
    factor_of = 1.0
    for position, shards_of in shards:
        draws = jax.random.uniform(jax.random.fold_in(jax.random.fold_in(stream_key, 6), position), (shards_of,), jnp.float32, least / len(shards), high / len(shards))
        factor_of = factor_of * jnp.repeat(jnp.exp(draws), dims[position] // shards_of).reshape((-1,) + (1,) * (len(dims) - 1 - position))
    return factor_of


def shared_out(own_key, own, number, rows, amount, top, limit, lean):
    ranking = jax.random.permutation(own_key, amount)
    heavy_load, ordinary = shares(amount, rows * top, limit, lean, True), shares(amount, rows * top, limit, lean, False)
    places = jnp.arange(amount)

    def named(lengths, turn):
        used = int((lengths > 0).sum())
        fixed = max(1, used // 4)
        moved = fixed + (places - fixed + turn * (used - fixed)) % max(1, amount - fixed)
        return jnp.zeros((amount,), jnp.int32).at[ranking[jnp.where(places < fixed, places, moved)]].set(jnp.asarray(lengths, jnp.int32))

    lengths = jnp.where(number % 4 == 0, named(heavy_load, number // 4), named(ordinary, number - number // 4 - 1))
    mixed = jax.random.permutation(jax.random.fold_in(own, 3), amount)
    source_of, sink = mixed[0:amount // 2 * 2:2], mixed[1:amount // 2 * 2:2]
    room = jnp.minimum(lengths[source_of] - 1, limit - lengths[sink]) // 2
    room = jnp.where((source_of == ranking[0]) | (sink == ranking[0]) | (lengths[sink] == 0), 0, jnp.maximum(room, 0))
    moved = jax.random.randint(jax.random.fold_in(own, 4), (amount // 2,), 0, 1 << 20) % (room + 1)
    lengths = lengths.at[source_of].add(-moved).at[sink].add(moved)
    members = jnp.searchsorted(jnp.cumsum(lengths), jnp.arange(rows * top), side="right").astype(jnp.int32)
    listing = members.reshape(top, rows).T
    listing = listing[jax.random.permutation(jax.random.fold_in(own, 1), rows)]
    turn = jax.random.randint(jax.random.fold_in(own, 2), (rows, 1), 0, top)
    return jnp.take_along_axis(listing, (jnp.arange(top)[None, :] + turn) % top, axis=1)


def shares(count, total, limit, skew, full):
    portions = [(1 << 20) // math.isqrt(grade ** skew) + 1 for grade in range(1, count + 1)]
    largest = limit if full else min(limit, max(-(-total // count), total * portions[0] // sum(portions)))
    least = 1 if total - largest >= count - 1 else 0
    counts, surplus = [largest] + [least] * (count - 1), total - largest - least * (count - 1)
    while surplus > 0:
        movable = [i for i in range(1, count) if counts[i] < largest] or [i for i in range(1, count) if counts[i] < limit]
        pool, remaining = sum([portions[i] for i in movable]), surplus
        for i in movable:
            more = min(limit - counts[i], max(1, remaining * portions[i] // pool), surplus)
            counts[i] = counts[i] + more
            surplus = surplus - more
    return np.array(counts)


def normal_values(stream_key, extent, spread, most, pieces=(), held_as=jnp.bfloat16):
    values = spread * jax.random.normal(stream_key, extent, jnp.float32)
    if pieces:
        values = values * shard_levels(stream_key, extent, pieces, -0.22, 0.18)
    return jnp.clip(values, -most, most).astype(held_as)


def setup_inputs(seed: int = 0) -> dict:
    streams_of = jax.random.split(jax.random.key(seed), 8)
    inputs = normal_values(streams_of[0], (MICRO, TOKENS, D), 1.0, 6.0, ((1, 64),))
    routes_keys = jax.random.split(jax.random.fold_in(streams_of[1], 1), N_SECTION * MICRO * TOKENS // TOK_MB)
    routes_turns = jax.random.permutation(jax.random.fold_in(streams_of[1], 3), N_SECTION * MICRO * TOKENS // TOK_MB)
    routes = jax.vmap(lambda own, number: shared_out(jax.random.fold_in(streams_of[1], 2), own, number, TOK_MB, E, 2, MOST, 1))(routes_keys, routes_turns).reshape((N_SECTION, MICRO, TOKENS, 2))
    norm_gain = jnp.clip(1.0 + 0.1 * jax.random.normal(streams_of[2], (N_SECTION, D), jnp.float32), 0.5, 1.5)
    router = normal_values(streams_of[3], (N_SECTION, D, E), D ** -0.5, 0.109375, ((0, 4),))
    w_gate = normal_values(streams_of[4], (N_SECTION, D, E * FF), D ** -0.5, 0.109375, ((0, 4), (2, 64)))
    w_up = normal_values(streams_of[5], (N_SECTION, D, E * FF), D ** -0.5, 0.109375, ((0, 4), (2, 64)))
    w_down = normal_values(streams_of[6], (N_SECTION, E * FF, D), FF ** -0.5, 0.0625, ((0, 4), (1, 64)))
    return dict(inputs=inputs, routes=routes, norm_gain=norm_gain, router=router, w_gate=w_gate, w_up=w_up, w_down=w_down)


EPSILON = 1e-05

def slot_table(route_ids, experts, capacity):
    flat_ids = route_ids.reshape(-1)
    onehot = (flat_ids[:, None] == jnp.arange(experts, dtype=jnp.int32)[None, :]).astype(jnp.int32)
    before = jnp.cumsum(onehot, axis=0) - onehot
    within = lax.optimization_barrier(jnp.sum(before * onehot, axis=1))
    target = (flat_ids * capacity + within).astype(jnp.int32)
    slot_grid = jnp.arange(experts * capacity, dtype=jnp.int32)[:, None] == target[None, :]
    return (target, slot_grid)

def normalize(hidden, gain_row):
    wide_hidden = hidden.astype(jnp.float32)
    inv_rms = lax.rsqrt(lax.optimization_barrier(jnp.mean(wide_hidden * wide_hidden, axis=-1, keepdims=True)) + EPSILON)
    normed = (wide_hidden * inv_rms * gain_row).astype(jnp.bfloat16)
    return (wide_hidden, inv_rms, normed)

def first_share(normed, router, route_ids):
    logits = jnp.dot(normed, router, preferred_element_type=jnp.float32)
    match_mask = route_ids[:, :, None] == jnp.arange(router.shape[1], dtype=jnp.int32)[None, None, :]
    chosen = lax.optimization_barrier(jnp.sum(jnp.where(match_mask, logits[:, None, :], 0.0), axis=-1))
    return jax.nn.sigmoid(chosen[:, 0] - chosen[:, 1])

def dispatch_rows(route_rows, tables):
    placed = jnp.einsum('nqr,nrd->nqd', tables.astype(jnp.float32), route_rows.astype(jnp.float32), precision=lax.Precision.HIGHEST)
    return placed.astype(jnp.bfloat16)

def take_rows(summed, target):
    return jnp.take(summed, target, axis=0)

def expert_forward(row_block, gate_mat, up_mat, down_mat):
    rows_wide = row_block.astype(jnp.float32)
    gate_value = jnp.einsum('qd,dgf->gqf', rows_wide, gate_mat.astype(jnp.float32), precision=lax.Precision.HIGHEST)
    up_value = jnp.einsum('qd,dgf->gqf', rows_wide, up_mat.astype(jnp.float32), precision=lax.Precision.HIGHEST)
    hidden = (jax.nn.silu(gate_value) * up_value).astype(jnp.bfloat16)
    partial_out = jnp.einsum('gqf,gfd->gqd', hidden.astype(jnp.float32), down_mat.astype(jnp.float32), precision=lax.Precision.HIGHEST)
    return lax.optimization_barrier(jnp.sum(partial_out.astype(jnp.bfloat16).astype(jnp.float32), axis=0))

def split_weights(gate_all, up_all, down_all):
    groups = N_EXPERT // E
    return (gate_all.reshape(D, E, groups, FF_DEV), up_all.reshape(D, E, groups, FF_DEV), down_all.reshape(E, groups, FF_DEV, D))

def layer_forward(hidden, route_ids, gain_row, router, gate_all, up_all, down_all):
    wide_hidden, inv_rms, normed = normalize(hidden, gain_row)
    share = first_share(normed, router, route_ids)
    targets, tables = jax.vmap(partial(slot_table, experts=E, capacity=MOST))(route_ids.reshape(N_EXPERT, TOK_MB, 2))
    route_rows = jnp.repeat(normed, 2, axis=0).reshape(N_EXPERT, TOK_MB * 2, D)
    outgoing = dispatch_rows(route_rows, tables).reshape(N_EXPERT, E, MOST, D)
    gate_split, up_split, down_split = split_weights(gate_all, up_all, down_all)
    totals = []
    for expert_id in range(E):
        block_rows = outgoing[:, expert_id].reshape(N_EXPERT * MOST, D)
        totals.append(expert_forward(block_rows, gate_split[:, expert_id], up_split[:, expert_id], down_split[expert_id]).reshape(N_EXPERT, MOST, D))
    summed = jnp.stack(totals, axis=1).reshape(N_EXPERT, E * MOST, D)
    routed = jax.vmap(take_rows)(summed, targets).reshape(N_EXPERT * TOK_MB, 2, D)
    result = wide_hidden + share[:, None] * routed[:, 0] + (1.0 - share)[:, None] * routed[:, 1]
    return result.astype(jnp.bfloat16)

def reference(inputs, routes, norm_gain, router, w_gate, w_up, w_down):
    outputs = [[] for section_id in range(N_SECTION)]
    for micro_id in range(MICRO):
        hidden = inputs[micro_id]
        for section_id in range(N_SECTION):
            hidden = layer_forward(hidden, routes[section_id, micro_id], norm_gain[section_id], router[section_id], w_gate[section_id], w_up[section_id], w_down[section_id])
            outputs[section_id].append(hidden)
    return jnp.stack([jnp.stack(items) for items in outputs])
```

```python
import jax
import jax.numpy as jnp
from jax import lax
from jax.sharding import PartitionSpec as P

E = 4
MOST = 2
PAIR = 2
EPSILON = 1e-05

SLICES = [[e * 16 + j * 2 + c for j in range(8)] for e in range(E) for c in range(2)]
EXPERTS = [[e * 16 + r for e in range(E)] for r in range(16)]
CORES = [(i, i ^ 1) for i in range(64)]


def gather_over(block, groups, count):
    copies = jnp.broadcast_to(block[None], (count,) + block.shape)
    return lax.all_to_all(
        copies, "expert", split_axis=0, concat_axis=0, axis_index_groups=groups, tiled=True
    )


def tables(ids, expert):
    pairs, tokens = ids.shape[0], ids.shape[3]
    blocks = PAIR * E
    flat = ids.reshape(pairs, blocks, tokens * 2)
    same = flat[..., :, None] == flat[..., None, :]
    earlier = jnp.arange(tokens * 2)[:, None] > jnp.arange(tokens * 2)[None, :]
    slot = jnp.sum((same & earlier).astype(jnp.int32), axis=-1)
    block = jnp.arange(blocks, dtype=jnp.int32)[None, :, None]
    row = block * MOST + slot
    rows = blocks * MOST
    mine = jnp.where(flat == expert, row, -1).reshape(pairs, 1, blocks * tokens, 2)
    pick = jnp.any(mine == jnp.arange(rows, dtype=jnp.int32)[None, :, None, None], axis=-1)
    back = (flat * rows + row).reshape(pairs, blocks * tokens, 2)
    back = jnp.swapaxes(back, 1, 2).reshape(pairs, 2 * blocks * tokens, 1)
    place = back == jnp.arange(E * rows, dtype=jnp.int32)[None, None, :]
    return pick.astype(jnp.bfloat16), place.astype(jnp.bfloat16)


def on_device(inputs, routes, norm_gain, router, w_gate, w_up, w_down):
    sections = lax.axis_size("section")
    section_pos = lax.axis_index("section")
    member_pos = lax.axis_index("expert")
    expert, rest = member_pos // 16, member_pos % 16
    micro_count, tokens, width = inputs.shape
    pairs = micro_count // PAIR
    held = PAIR * E * tokens
    gain_row, router_mat = norm_gain[0], router[0]
    gate_mat, up_mat, down_mat = w_gate[0], w_up[0], w_down[0]

    def ffn(rows):
        gate_value = jnp.dot(rows, gate_mat, preferred_element_type=jnp.float32)
        up_value = jnp.dot(rows, up_mat, preferred_element_type=jnp.float32)
        hidden = (jax.nn.silu(gate_value) * up_value).astype(jnp.bfloat16)
        return jnp.dot(hidden, down_mat, preferred_element_type=jnp.float32).astype(jnp.bfloat16)

    ids = routes[0].reshape(pairs, PAIR, E, 16, tokens, 2)
    ids = lax.dynamic_index_in_dim(ids, rest, 3, keepdims=False)
    pick_all, place_all = tables(ids, expert)
    ids_all = ids.reshape(pairs, held, 2)

    entering = gather_over(inputs.reshape(micro_count * tokens, width), EXPERTS, E)
    entering = entering.reshape(E, pairs, PAIR, tokens, width)
    entering = jnp.transpose(entering, (1, 2, 0, 3, 4)).reshape(pairs, held, width)

    arriving = jnp.zeros((held, width), jnp.bfloat16)
    kept = []
    for tick in range(pairs + sections - 1):
        pair = jnp.clip(tick - section_pos, 0, pairs - 1)
        pick = lax.dynamic_index_in_dim(pick_all, pair, 0, keepdims=False)
        place = lax.dynamic_index_in_dim(place_all, pair, 0, keepdims=False)
        route_ids = lax.dynamic_index_in_dim(ids_all, pair, 0, keepdims=False)
        hidden = jnp.where(section_pos == 0, entering[min(tick, pairs - 1)], arriving)
        wide = hidden.astype(jnp.float32)
        inv_rms = lax.rsqrt(jnp.mean(wide * wide, axis=-1, keepdims=True) + EPSILON)
        normed = (wide * inv_rms * gain_row).astype(jnp.bfloat16)
        sent = jnp.dot(pick, normed, preferred_element_type=jnp.float32).astype(jnp.bfloat16)
        own = gather_over(sent, SLICES, 8).reshape(8 * sent.shape[0], width)
        other = lax.ppermute(own, "expert", CORES)
        other_out = lax.ppermute(ffn(other), "expert", CORES)
        own_out = ffn(own)
        both = (own_out.astype(jnp.float32) + other_out.astype(jnp.float32)).astype(jnp.bfloat16)
        parts = lax.all_to_all(
            both.reshape(8, sent.shape[0], width),
            "expert",
            split_axis=0,
            concat_axis=0,
            axis_index_groups=SLICES,
            tiled=True,
        )
        expert_out = jnp.sum(parts.astype(jnp.float32), axis=0).astype(jnp.bfloat16)
        outs = gather_over(expert_out, EXPERTS, E).reshape(E * sent.shape[0], width)
        logits = jnp.dot(normed, router_mat, preferred_element_type=jnp.float32)
        match = route_ids[:, :, None] == jnp.arange(E, dtype=jnp.int32)[None, None, :]
        chosen = jnp.sum(jnp.where(match, logits[:, None, :], 0.0), axis=-1)
        share = jax.nn.sigmoid(chosen[:, 0] - chosen[:, 1])[:, None]
        routed = jnp.dot(place, outs, preferred_element_type=jnp.float32)
        result = (wide + share * routed[:held] + (1.0 - share) * routed[held:]).astype(jnp.bfloat16)
        mine = lax.dynamic_index_in_dim(
            result.reshape(PAIR, E, tokens, width), expert, 1, keepdims=False
        )
        kept.append(mine)
        if tick + 1 < pairs + sections - 1:
            arriving = lax.ppermute(
                result, "section", [(i, i + 1) for i in range(sections - 1)]
            )
    stored = lax.dynamic_slice_in_dim(jnp.stack(kept), section_pos, pairs, 0)
    return stored.reshape(1, micro_count, tokens, width)


def solution(mesh):
    placed = (
        P(None, "expert", None),
        P("section", None, None, None),
        P("section", None),
        P("section", None, None),
        P("section", None, "expert"),
        P("section", None, "expert"),
        P("section", "expert", None),
    )
    return jax.shard_map(
        on_device,
        mesh=mesh,
        in_specs=placed,
        out_specs=P("section", None, "expert", None),
        check_vma=False,
    )
```

```python
import jax
import jax.numpy as jnp
from jax import lax
from jax.sharding import PartitionSpec as P

E = 4
MOST = 2
PAIR = 2
SHARERS = 8
EPSILON = 1e-05

SLICES = [[e * 16 + j * 2 + c for j in range(8)] for e in range(E) for c in range(2)]
EXPERTS = [[e * 16 + r for e in range(E)] for r in range(16)]
CORES = [(i, i ^ 1) for i in range(64)]


def exchange(block, groups, count):
    rows = block.shape[0] // count
    chunks = block.reshape(count, rows, block.shape[1])
    moved = lax.all_to_all(
        chunks, "expert", split_axis=0, concat_axis=0, axis_index_groups=groups, tiled=True
    )
    return moved.reshape(block.shape)


def choose(picks, rows):
    return jnp.dot(picks, rows, preferred_element_type=jnp.float32)


def tables(ids, expert):
    pairs, tokens = ids.shape[0], ids.shape[3]
    blocks = PAIR * E
    flat = ids.reshape(pairs, blocks, tokens * 2)
    same = flat[..., :, None] == flat[..., None, :]
    earlier = jnp.arange(tokens * 2)[:, None] > jnp.arange(tokens * 2)[None, :]
    slot = jnp.sum((same & earlier).astype(jnp.int32), axis=-1)
    block = jnp.arange(blocks, dtype=jnp.int32)[None, :, None]
    row = block * MOST + slot
    rows = blocks * MOST
    mine = jnp.where(flat == expert, row, -1).reshape(pairs, 1, blocks * tokens, 2)
    wanted = jnp.arange(SHARERS * rows, dtype=jnp.int32)[None, :, None, None] % rows
    pick = jnp.any(mine == wanted, axis=-1)
    back = (flat * rows + row).reshape(pairs, blocks * tokens, 2)
    back = jnp.swapaxes(back, 1, 2).reshape(pairs, 2 * blocks * tokens, 1)
    place = back == jnp.arange(E * rows, dtype=jnp.int32)[None, None, :]
    named = ids.reshape(pairs, blocks * tokens, 2)[..., None] == jnp.arange(E, dtype=jnp.int32)
    sign = named[:, :, 0].astype(jnp.float32) - named[:, :, 1].astype(jnp.float32)
    return pick.astype(jnp.bfloat16), place.astype(jnp.bfloat16), sign


def on_device(inputs, routes, norm_gain, router, w_gate, w_up, w_down):
    barrier = lax.optimization_barrier
    sections = lax.axis_size("section")
    section_pos = lax.axis_index("section")
    member_pos = lax.axis_index("expert")
    expert, rest = member_pos // 16, member_pos % 16
    micro_count, tokens, width = inputs.shape
    pairs = micro_count // PAIR
    held = PAIR * E * tokens
    sent_rows = PAIR * E * MOST
    ticks = pairs + sections - 1
    gain_row, router_mat = norm_gain[0], router[0]
    gate_mat, up_mat, down_mat = w_gate[0], w_up[0], w_down[0]

    def hidden_units(rows):
        gate_value = jnp.dot(rows, gate_mat, preferred_element_type=jnp.float32)
        up_value = jnp.dot(rows, up_mat, preferred_element_type=jnp.float32)
        gate_value, up_value = barrier((gate_value, up_value))
        return barrier((jax.nn.silu(gate_value) * up_value).astype(jnp.bfloat16))

    def project(units):
        return barrier(
            jnp.dot(units, down_mat, preferred_element_type=jnp.float32).astype(jnp.bfloat16)
        )

    ids = routes[0].reshape(pairs, PAIR, E, 16, tokens, 2)
    ids = lax.dynamic_index_in_dim(ids, rest, 3, keepdims=False)
    pick_all, place_all, sign_all = tables(ids, expert)

    spare = 16
    own_rows = jnp.swapaxes(inputs, 0, 1).reshape(tokens * micro_count, width)
    lay_out = (
        jnp.arange(E * spare, dtype=jnp.int32)[:, None] % spare
        == jnp.arange(tokens * micro_count, dtype=jnp.int32)[None, :]
    ).astype(jnp.bfloat16)
    entering = exchange(choose(lay_out, own_rows).astype(jnp.bfloat16), EXPERTS, E)
    spot = jnp.arange(held, dtype=jnp.int32)
    spot_micro, spot_block, spot_token = (
        spot // (E * tokens),
        spot // tokens % E,
        spot % tokens,
    )

    def entrance(pair):
        source = spot_block * spare + spot_token * micro_count + pair * PAIR + spot_micro
        picks = source[:, None] == jnp.arange(E * spare, dtype=jnp.int32)[None, :]
        return choose(picks.astype(jnp.bfloat16), entering).astype(jnp.bfloat16)

    total = jnp.arange(E * sent_rows, dtype=jnp.int32)[:, None] % sent_rows
    total = total == jnp.arange(SHARERS * sent_rows, dtype=jnp.int32)[None, :] % sent_rows
    total = total.astype(jnp.bfloat16)

    arriving = jnp.zeros((held, width), jnp.bfloat16)
    stored = jnp.zeros((16, width), jnp.float32)
    for tick in range(ticks):
        due = tick - section_pos
        pair = jnp.clip(due, 0, pairs - 1)
        pick = lax.dynamic_index_in_dim(pick_all, pair, 0, keepdims=False)
        place = lax.dynamic_index_in_dim(place_all, pair, 0, keepdims=False)
        sign = lax.dynamic_index_in_dim(sign_all, pair, 0, keepdims=False)
        hidden = jnp.where(section_pos == 0, entrance(min(tick, pairs - 1)), arriving)
        hidden = barrier(hidden)
        wide = hidden.astype(jnp.float32)
        inv_rms = lax.rsqrt(jnp.mean(wide * wide, axis=-1, keepdims=True) + EPSILON)
        normed = barrier((wide * inv_rms * gain_row).astype(jnp.bfloat16))
        own = exchange(choose(pick, normed).astype(jnp.bfloat16), SLICES, SHARERS)
        other = lax.ppermute(own, "expert", CORES)
        own_units = hidden_units(own)
        other_out = lax.ppermute(project(hidden_units(other)), "expert", CORES)
        own_out = project(own_units)
        both = (own_out.astype(jnp.float32) + other_out.astype(jnp.float32)).astype(jnp.bfloat16)
        logits = jnp.dot(normed, router_mat, preferred_element_type=jnp.float32)
        share = jax.nn.sigmoid(jnp.sum(logits * sign, axis=-1, keepdims=True))
        both, share, rest_share = barrier((both, share, 1.0 - share))
        parts = exchange(both, SLICES, SHARERS)
        outs = exchange(choose(total, parts).astype(jnp.bfloat16), EXPERTS, E)
        routed = choose(place, outs)
        result = (wide + share * routed[:held] + rest_share * routed[held:]).astype(jnp.bfloat16)
        result = barrier(result)
        if tick + 1 < ticks:
            arriving = lax.ppermute(
                result, "section", [(i, i + 1) for i in range(sections - 1)]
            )
        target = (pair * PAIR + spot_micro) * 4 + spot_token
        target = jnp.where((spot_block == expert) & (due == pair), target, -1)
        keep = target[None, :] == jnp.arange(16, dtype=jnp.int32)[:, None]
        stored = stored + choose(keep.astype(jnp.bfloat16), result)
    stored = stored.astype(jnp.bfloat16).reshape(1, micro_count, 4, width)
    return stored[:, :, :tokens]


def solution(mesh):
    placed = (
        P(None, "expert", None),
        P("section", None, None, None),
        P("section", None),
        P("section", None, None),
        P("section", None, "expert"),
        P("section", None, "expert"),
        P("section", "expert", None),
    )
    return jax.shard_map(
        on_device,
        mesh=mesh,
        in_specs=placed,
        out_specs=P("section", None, "expert", None),
        check_vma=False,
    )
```

```python
import jax
import jax.numpy as jnp
from jax import lax
from jax.sharding import PartitionSpec as P

E = 4
MOST = 2
PAIR = 2
SHARERS = 8
EPSILON = 1e-05

SLICES = [[e * 16 + j * 2 + c for j in range(8)] for e in range(E) for c in range(2)]
EXPERTS = [[e * 16 + r for e in range(E)] for r in range(16)]
CORES = [(i, i ^ 1) for i in range(64)]


def exchange(block, groups, count):
    rows = block.shape[0] // count
    chunks = block.reshape(count, rows, block.shape[1])
    moved = lax.all_to_all(
        chunks, "expert", split_axis=0, concat_axis=0, axis_index_groups=groups, tiled=True
    )
    return moved.reshape(block.shape)


def choose(picks, rows):
    return jnp.dot(picks, rows, preferred_element_type=jnp.float32)


def tables(route_all, expert, rest, tokens):
    micro_count, requests, _ = route_all.shape
    rows = PAIR * E * MOST
    spots = micro_count * E * tokens

    def column(values):
        return values[:, None]

    spot = jnp.arange(spots, dtype=jnp.int32)
    micro, block, token = spot // (E * tokens), spot // tokens % E, spot % tokens
    seat = (block * (requests // E // tokens) + rest) * tokens + token
    seats = column(seat) == jnp.arange(requests, dtype=jnp.int32)[None, :]
    listed = jnp.transpose(route_all, (0, 2, 1)).reshape(2 * micro_count, requests)
    named = lax.dot_general(
        seats.astype(jnp.bfloat16),
        listed.astype(jnp.bfloat16),
        (((1,), (1,)), ((), ())),
        preferred_element_type=jnp.float32,
    )
    at = jnp.arange(2 * micro_count, dtype=jnp.int32)[None, :]
    first = jnp.sum(jnp.where(at == 2 * column(micro), named, 0.0), axis=1, keepdims=True)
    second = jnp.sum(jnp.where(at == 2 * column(micro) + 1, named, 0.0), axis=1, keepdims=True)
    first, second = lax.optimization_barrier((first, second))
    first, second = first.astype(jnp.int32), second.astype(jnp.int32)
    group = spot // tokens
    earlier = (column(group) == group[None, :]) & (column(spot) > spot[None, :])
    earlier = earlier.astype(jnp.bfloat16)
    begin = column(group % (PAIR * E)) * MOST

    def slots(hits, lanes):
        before = jnp.dot(earlier, hits.astype(jnp.bfloat16), preferred_element_type=jnp.float32)
        return before.astype(jnp.int32) == lanes[None, :] % rows - begin

    lanes = jnp.arange(SHARERS * rows, dtype=jnp.int32)
    hits = jnp.broadcast_to((first == expert) | (second == expert), (spots, SHARERS * rows))
    pick = (hits & slots(hits, lanes)).astype(jnp.bfloat16)
    lanes = jnp.arange(E * rows, dtype=jnp.int32)
    first_hit = first == lanes[None, :] // rows
    second_hit = second == lanes[None, :] // rows
    fits = slots(first_hit | second_hit, lanes)
    place = [(hit & fits).astype(jnp.bfloat16) for hit in (first_hit, second_hit)]
    ids = jnp.arange(E, dtype=jnp.int32)[None, :]
    sign = (first == ids).astype(jnp.float32) - (second == ids).astype(jnp.float32)
    return lax.optimization_barrier((pick, place[0], place[1], sign))


def on_device(inputs, routes, norm_gain, router, w_gate, w_up, w_down):
    barrier = lax.optimization_barrier
    sections = lax.axis_size("section")
    section_pos = lax.axis_index("section")
    member_pos = lax.axis_index("expert")
    expert, rest = member_pos // 16, member_pos % 16
    micro_count, tokens, width = inputs.shape
    pairs = micro_count // PAIR
    held = PAIR * E * tokens
    sent_rows = PAIR * E * MOST
    ticks = pairs + sections - 1
    gain_row, router_mat = norm_gain[0], router[0]
    gate_mat, up_mat, down_mat = w_gate[0], w_up[0], w_down[0]

    def hidden_units(rows):
        gate_value = jnp.dot(rows, gate_mat, preferred_element_type=jnp.float32)
        up_value = jnp.dot(rows, up_mat, preferred_element_type=jnp.float32)
        gate_value, up_value = barrier((gate_value, up_value))
        return barrier((jax.nn.silu(gate_value) * up_value).astype(jnp.bfloat16))

    def project(units):
        return barrier(
            jnp.dot(units, down_mat, preferred_element_type=jnp.float32).astype(jnp.bfloat16)
        )

    pick_all, first_all, second_all, sign_all = tables(routes[0], expert, rest, tokens)

    spare = 16
    own_rows = jnp.swapaxes(inputs, 0, 1).reshape(tokens * micro_count, width)
    lay_out = (
        jnp.arange(E * spare, dtype=jnp.int32)[:, None] % spare
        == jnp.arange(tokens * micro_count, dtype=jnp.int32)[None, :]
    ).astype(jnp.bfloat16)
    entering = exchange(choose(lay_out, own_rows).astype(jnp.bfloat16), EXPERTS, E)
    spot = jnp.arange(held, dtype=jnp.int32)
    spot_micro, spot_block, spot_token = (
        spot // (E * tokens),
        spot // tokens % E,
        spot % tokens,
    )

    def entrance(pair, entering):
        source = spot_block * spare + spot_token * micro_count + pair * PAIR + spot_micro
        picks = source[:, None] == jnp.arange(E * spare, dtype=jnp.int32)[None, :]
        return choose(picks.astype(jnp.bfloat16), entering).astype(jnp.bfloat16)

    total = jnp.arange(E * sent_rows, dtype=jnp.int32)[:, None] % sent_rows
    total = total == jnp.arange(SHARERS * sent_rows, dtype=jnp.int32)[None, :] % sent_rows
    total = total.astype(jnp.bfloat16)

    entry = entrance(0, entering)
    arriving = jnp.zeros((held, width), jnp.bfloat16)
    stored = jnp.zeros((16, width), jnp.float32)
    for tick in range(ticks):
        due = tick - section_pos
        pair = jnp.clip(due, 0, pairs - 1)
        pick, first_place, second_place, sign = (
            lax.dynamic_slice_in_dim(table, pair * held, held, 0)
            for table in (pick_all, first_all, second_all, sign_all)
        )
        hidden = jnp.where(section_pos == 0, entry, arriving)
        hidden = barrier(hidden)
        wide = hidden.astype(jnp.float32)
        inv_rms = lax.rsqrt(jnp.mean(wide * wide, axis=-1, keepdims=True) + EPSILON)
        normed = barrier((wide * inv_rms * gain_row).astype(jnp.bfloat16))
        sent = lax.dot_general(
            pick, normed, (((0,), (0,)), ((), ())), preferred_element_type=jnp.float32
        ).astype(jnp.bfloat16)
        if tick == 0:
            sent, first_all, second_all, sign_all, total = barrier(
                (sent, first_all, second_all, sign_all, total)
            )
        own = exchange(sent, SLICES, SHARERS)
        other = lax.ppermute(own, "expert", CORES)
        own_units = hidden_units(own)
        other_out = lax.ppermute(project(hidden_units(other)), "expert", CORES)
        own_out = project(own_units)
        both = (own_out.astype(jnp.float32) + other_out.astype(jnp.float32)).astype(jnp.bfloat16)
        logits = jnp.dot(normed, router_mat, preferred_element_type=jnp.float32)
        share = jax.nn.sigmoid(jnp.sum(logits * sign, axis=-1, keepdims=True))
        both, share, rest_share = barrier((both, share, 1.0 - share))
        parts = exchange(both, SLICES, SHARERS)
        outs = exchange(choose(total, parts).astype(jnp.bfloat16), EXPERTS, E)
        first_out, second_out = choose(first_place, outs), choose(second_place, outs)
        result = (wide + share * first_out + rest_share * second_out).astype(jnp.bfloat16)
        result, entering, due = barrier((result, entering, due))
        if tick + 1 < ticks:
            arriving = lax.ppermute(
                result, "section", [(i, i + 1) for i in range(sections - 1)]
            )
        if tick + 1 < pairs:
            entry = entrance(tick + 1, entering)
        target = (due * PAIR + spot_micro) * 4 + spot_token
        held_now = (spot_block == expert) & (due >= 0) & (due < pairs)
        target = jnp.where(held_now, target, -1)
        keep = target[None, :] == jnp.arange(16, dtype=jnp.int32)[:, None]
        stored = stored + choose(keep.astype(jnp.bfloat16), result)
        if tick + 1 < ticks:
            arriving, stored, entry = barrier((arriving, stored, entry))
    stored = stored.astype(jnp.bfloat16).reshape(1, micro_count, 4, width)
    return stored[:, :, :tokens]


def solution(mesh):
    placed = (
        P(None, "expert", None),
        P("section", None, None, None),
        P("section", None),
        P("section", None, None),
        P("section", None, "expert"),
        P("section", None, "expert"),
        P("section", "expert", None),
    )
    return jax.shard_map(
        on_device,
        mesh=mesh,
        in_specs=placed,
        out_specs=P("section", None, "expert", None),
        check_vma=False,
    )
```

```python
import jax
import jax.numpy as jnp
from jax import lax
from jax.sharding import PartitionSpec as P

E = 4
MOST = 2
PAIR = 2
SHARERS = 8
EPSILON = 1e-05

SLICES = [[e * 16 + j * 2 + c for j in range(8)] for e in range(E) for c in range(2)]
EXPERTS = [[e * 16 + r for e in range(E)] for r in range(16)]
CORES = [(i, i ^ 1) for i in range(64)]


def exchange(block, groups, count):
    rows = block.shape[0] // count
    chunks = block.reshape(count, rows, block.shape[1])
    moved = lax.all_to_all(
        chunks, "expert", split_axis=0, concat_axis=0, axis_index_groups=groups, tiled=True
    )
    return moved.reshape(block.shape)


def choose(picks, rows):
    return jnp.dot(picks, rows, preferred_element_type=jnp.float32)


def tables(route_all, expert, rest, tokens):
    micro_count, requests, _ = route_all.shape
    rows = PAIR * E * MOST
    spots = micro_count * E * tokens

    def column(values):
        return values[:, None]

    spot = jnp.arange(spots, dtype=jnp.int32)
    micro, block, token = spot // (E * tokens), spot // tokens % E, spot % tokens
    seat = (block * (requests // E // tokens) + rest) * tokens + token
    seats = column(seat) == jnp.arange(requests, dtype=jnp.int32)[None, :]
    listed = jnp.transpose(route_all, (0, 2, 1)).reshape(2 * micro_count, requests)
    named = lax.dot_general(
        seats.astype(jnp.bfloat16),
        listed.astype(jnp.bfloat16),
        (((1,), (1,)), ((), ())),
        preferred_element_type=jnp.float32,
    )
    at = jnp.arange(2 * micro_count, dtype=jnp.int32)[None, :]
    first = jnp.sum(jnp.where(at == 2 * column(micro), named, 0.0), axis=1, keepdims=True)
    second = jnp.sum(jnp.where(at == 2 * column(micro) + 1, named, 0.0), axis=1, keepdims=True)
    first, second = lax.optimization_barrier((first, second))
    first, second = first.astype(jnp.int32), second.astype(jnp.int32)
    group = spot // tokens
    earlier = (column(group) == group[None, :]) & (column(spot) > spot[None, :])
    earlier = earlier.astype(jnp.bfloat16)
    begin = column(group % (PAIR * E)) * MOST

    def slots(hits, lanes):
        before = jnp.dot(earlier, hits.astype(jnp.bfloat16), preferred_element_type=jnp.float32)
        return before.astype(jnp.int32) == lanes[None, :] % rows - begin

    lanes = jnp.arange(SHARERS * rows, dtype=jnp.int32)
    hits = jnp.broadcast_to((first == expert) | (second == expert), (spots, SHARERS * rows))
    pick = (hits & slots(hits, lanes)).astype(jnp.bfloat16)
    lanes = jnp.arange(E * rows, dtype=jnp.int32)
    first_hit = first == lanes[None, :] // rows
    second_hit = second == lanes[None, :] // rows
    fits = slots(first_hit | second_hit, lanes)
    place = [(hit & fits).astype(jnp.bfloat16) for hit in (first_hit, second_hit)]
    ids = jnp.arange(E, dtype=jnp.int32)[None, :]
    sign = (first == ids).astype(jnp.float32) - (second == ids).astype(jnp.float32)
    return lax.optimization_barrier((pick, place[0], place[1], sign))


def on_device(inputs, routes, norm_gain, router, w_gate, w_up, w_down):
    barrier = lax.optimization_barrier
    sections = lax.axis_size("section")
    section_pos = lax.axis_index("section")
    member_pos = lax.axis_index("expert")
    expert, rest = member_pos // 16, member_pos % 16
    micro_count, tokens, width = inputs.shape
    pairs = micro_count // PAIR
    held = PAIR * E * tokens
    sent_rows = PAIR * E * MOST
    ticks = pairs + sections - 1
    gain_row, router_mat = norm_gain[0], router[0]
    gate_mat, up_mat, down_mat = w_gate[0], w_up[0], w_down[0]

    def hidden_units(rows):
        gate_value = jnp.dot(rows, gate_mat, preferred_element_type=jnp.float32)
        up_value = jnp.dot(rows, up_mat, preferred_element_type=jnp.float32)
        gate_value, up_value = barrier((gate_value, up_value))
        return barrier((jax.nn.silu(gate_value) * up_value).astype(jnp.bfloat16))

    def project(units):
        return barrier(
            jnp.dot(units, down_mat, preferred_element_type=jnp.float32).astype(jnp.bfloat16)
        )

    pick_all, first_all, second_all, sign_all = tables(routes[0], expert, rest, tokens)

    spare = 16
    own_rows = jnp.swapaxes(inputs, 0, 1).reshape(tokens * micro_count, width)
    lay_out = (
        jnp.arange(E * spare, dtype=jnp.int32)[:, None] % spare
        == jnp.arange(tokens * micro_count, dtype=jnp.int32)[None, :]
    ).astype(jnp.bfloat16)
    entering = exchange(choose(lay_out, own_rows).astype(jnp.bfloat16), EXPERTS, E)
    spot = jnp.arange(held, dtype=jnp.int32)
    spot_micro, spot_block, spot_token = (
        spot // (E * tokens),
        spot // tokens % E,
        spot % tokens,
    )

    def entrance(pair, entering):
        source = spot_block * spare + spot_token * micro_count + pair * PAIR + spot_micro
        picks = source[:, None] == jnp.arange(E * spare, dtype=jnp.int32)[None, :]
        return choose(picks.astype(jnp.bfloat16), entering).astype(jnp.bfloat16)

    total = jnp.arange(E * sent_rows, dtype=jnp.int32)[:, None] % sent_rows
    total = total == jnp.arange(SHARERS * sent_rows, dtype=jnp.int32)[None, :] % sent_rows
    total = total.astype(jnp.bfloat16)

    dues = [jnp.int32(tick) - section_pos for tick in range(ticks)]
    starts = [(jnp.clip(due, 0, pairs - 1) * held).astype(jnp.uint32) for due in dues]
    entry = entrance(0, entering)
    arriving = jnp.zeros((held, width), jnp.bfloat16)
    stored = jnp.zeros((16, width), jnp.float32)
    for tick in range(ticks):
        due, start = dues[tick], starts[tick]
        pick, first_place, second_place, sign = (
            lax.dynamic_slice_in_dim(table, start, held, 0)
            for table in (pick_all, first_all, second_all, sign_all)
        )
        hidden = jnp.where(section_pos == 0, entry, arriving)
        hidden = barrier(hidden)
        wide = hidden.astype(jnp.float32)
        inv_rms = lax.rsqrt(jnp.mean(wide * wide, axis=-1, keepdims=True) + EPSILON)
        normed = barrier((wide * inv_rms * gain_row).astype(jnp.bfloat16))
        sent = lax.dot_general(
            pick, normed, (((0,), (0,)), ((), ())), preferred_element_type=jnp.float32
        ).astype(jnp.bfloat16)
        if tick == 0:
            sent, first_all, second_all, sign_all, total, dues, starts = barrier(
                (sent, first_all, second_all, sign_all, total, dues, starts)
            )
        own = exchange(sent, SLICES, SHARERS)
        other = lax.ppermute(own, "expert", CORES)
        own_units = hidden_units(own)
        other_out = lax.ppermute(project(hidden_units(other)), "expert", CORES)
        own_out = project(own_units)
        both = (own_out.astype(jnp.float32) + other_out.astype(jnp.float32)).astype(jnp.bfloat16)
        logits = jnp.dot(normed, router_mat, preferred_element_type=jnp.float32)
        share = jax.nn.sigmoid(jnp.sum(logits * sign, axis=-1, keepdims=True))
        both, share, rest_share = barrier((both, share, 1.0 - share))
        parts = exchange(both, SLICES, SHARERS)
        outs = exchange(choose(total, parts).astype(jnp.bfloat16), EXPERTS, E)
        first_out, second_out = choose(first_place, outs), choose(second_place, outs)
        result = (wide + share * first_out + rest_share * second_out).astype(jnp.bfloat16)
        result, entering, due = barrier((result, entering, due))
        if tick + 1 < ticks:
            arriving = lax.ppermute(
                result, "section", [(i, i + 1) for i in range(sections - 1)]
            )
        if tick + 1 < pairs:
            entry = entrance(tick + 1, entering)
        target = (due * PAIR + spot_micro) * 4 + spot_token
        held_now = (spot_block == expert) & (due >= 0) & (due < pairs)
        target = jnp.where(held_now, target, -1)
        keep = target[None, :] == jnp.arange(16, dtype=jnp.int32)[:, None]
        stored = stored + choose(keep.astype(jnp.bfloat16), result)
        if tick + 1 < ticks:
            arriving, stored, entry = barrier((arriving, stored, entry))
    stored = stored.astype(jnp.bfloat16).reshape(1, micro_count, 4, width)
    return stored[:, :, :tokens]


def solution(mesh):
    placed = (
        P(None, "expert", None),
        P("section", None, None, None),
        P("section", None),
        P("section", None, None),
        P("section", None, "expert"),
        P("section", None, "expert"),
        P("section", "expert", None),
    )
    return jax.shard_map(
        on_device,
        mesh=mesh,
        in_specs=placed,
        out_specs=P("section", None, "expert", None),
        check_vma=False,
    )
```

```python
import jax
import jax.numpy as jnp
from jax import lax
from jax.sharding import PartitionSpec as P

E = 4
MOST = 2
PAIR = 2
SHARERS = 8
EPSILON = 1e-05

SLICES = [[e * 16 + j * 2 + c for j in range(8)] for e in range(E) for c in range(2)]
EXPERTS = [[e * 16 + r for e in range(E)] for r in range(16)]
CORES = [(i, i ^ 1) for i in range(64)]


def exchange(block, groups, count):
    rows = block.shape[0] // count
    chunks = block.reshape(count, rows, block.shape[1])
    moved = lax.all_to_all(
        chunks, "expert", split_axis=0, concat_axis=0, axis_index_groups=groups, tiled=True
    )
    return moved.reshape(block.shape)


def choose(picks, rows):
    return jnp.dot(picks, rows, preferred_element_type=jnp.float32)


def tables(route_all, expert, rest, tokens):
    micro_count, requests, _ = route_all.shape
    rows = PAIR * E * MOST
    spots = micro_count * E * tokens

    def column(values):
        return values[:, None]

    spot = jnp.arange(spots, dtype=jnp.int32)
    micro, block, token = spot // (E * tokens), spot // tokens % E, spot % tokens
    seat = (block * (requests // E // tokens) + rest) * tokens + token
    seats = column(seat) == jnp.arange(requests, dtype=jnp.int32)[None, :]
    listed = jnp.transpose(route_all, (0, 2, 1)).reshape(2 * micro_count, requests)
    named = lax.dot_general(
        seats.astype(jnp.bfloat16),
        listed.astype(jnp.bfloat16),
        (((1,), (1,)), ((), ())),
        preferred_element_type=jnp.float32,
    )
    at = jnp.arange(2 * micro_count, dtype=jnp.int32)[None, :]
    first = jnp.sum(jnp.where(at == 2 * column(micro), named, 0.0), axis=1, keepdims=True)
    second = jnp.sum(jnp.where(at == 2 * column(micro) + 1, named, 0.0), axis=1, keepdims=True)
    first, second = lax.optimization_barrier((first, second))
    first, second = first.astype(jnp.int32), second.astype(jnp.int32)
    group = spot // tokens
    earlier = (column(group) == group[None, :]) & (column(spot) > spot[None, :])
    earlier = earlier.astype(jnp.bfloat16)
    begin = column(group % (PAIR * E)) * MOST

    def slots(hits, lanes):
        before = jnp.dot(earlier, hits.astype(jnp.bfloat16), preferred_element_type=jnp.float32)
        return before.astype(jnp.int32) == lanes[None, :] % rows - begin

    lanes = jnp.arange(SHARERS * rows, dtype=jnp.int32)
    hits = jnp.broadcast_to((first == expert) | (second == expert), (spots, SHARERS * rows))
    pick = (hits & slots(hits, lanes)).astype(jnp.bfloat16)
    lanes = jnp.arange(E * rows, dtype=jnp.int32)
    first_hit = first == lanes[None, :] // rows
    second_hit = second == lanes[None, :] // rows
    fits = slots(first_hit | second_hit, lanes)
    place = [(hit & fits).astype(jnp.bfloat16) for hit in (first_hit, second_hit)]
    ids = jnp.arange(E, dtype=jnp.int32)[None, :]
    sign = (first == ids).astype(jnp.float32) - (second == ids).astype(jnp.float32)
    return lax.optimization_barrier((pick, place[0], place[1], sign))


def on_device(inputs, routes, norm_gain, router, w_gate, w_up, w_down):
    barrier = lax.optimization_barrier
    sections = lax.axis_size("section")
    section_pos = lax.axis_index("section")
    member_pos = lax.axis_index("expert")
    expert, rest = member_pos // 16, member_pos % 16
    micro_count, tokens, width = inputs.shape
    pairs = micro_count // PAIR
    held = PAIR * E * tokens
    sent_rows = PAIR * E * MOST
    ticks = pairs + sections - 1
    gain_row, router_mat = norm_gain[0], router[0]
    gate_mat, up_mat, down_mat = w_gate[0], w_up[0], w_down[0]

    def hidden_units(rows):
        gate_value = jnp.dot(rows, gate_mat, preferred_element_type=jnp.float32)
        up_value = jnp.dot(rows, up_mat, preferred_element_type=jnp.float32)
        gate_value, up_value = barrier((gate_value, up_value))
        return barrier((jax.nn.silu(gate_value) * up_value).astype(jnp.bfloat16))

    def project(units):
        return barrier(
            jnp.dot(units, down_mat, preferred_element_type=jnp.float32).astype(jnp.bfloat16)
        )

    pick_all, first_all, second_all, sign_all = tables(routes[0], expert, rest, tokens)

    spare = 16
    own_rows = jnp.swapaxes(inputs, 0, 1).reshape(tokens * micro_count, width)
    lay_out = (
        jnp.arange(E * spare, dtype=jnp.int32)[:, None] % spare
        == jnp.arange(tokens * micro_count, dtype=jnp.int32)[None, :]
    ).astype(jnp.bfloat16)
    entering = exchange(choose(lay_out, own_rows).astype(jnp.bfloat16), EXPERTS, E)
    spot = jnp.arange(held, dtype=jnp.int32)
    spot_micro, spot_block, spot_token = (
        spot // (E * tokens),
        spot // tokens % E,
        spot % tokens,
    )

    def entry_picks(pair):
        source = spot_block * spare + spot_token * micro_count + pair * PAIR + spot_micro
        picks = source[:, None] == jnp.arange(E * spare, dtype=jnp.int32)[None, :]
        return picks.astype(jnp.bfloat16)

    total = jnp.arange(E * sent_rows, dtype=jnp.int32)[:, None] % sent_rows
    total = total == jnp.arange(SHARERS * sent_rows, dtype=jnp.int32)[None, :] % sent_rows
    total = total.astype(jnp.bfloat16)

    dues = [jnp.int32(tick) - section_pos for tick in range(ticks)]
    starts = [(jnp.clip(due, 0, pairs - 1) * held).astype(jnp.uint32) for due in dues]
    entries = [entry_picks(pair) for pair in range(pairs)]
    entry = choose(entries[0], entering).astype(jnp.bfloat16)
    arriving = jnp.zeros((held, width), jnp.bfloat16)
    stored = jnp.zeros((16, width), jnp.float32)
    for tick in range(ticks):
        due, start = dues[tick], starts[tick]
        pick, first_place, second_place, sign = (
            lax.dynamic_slice_in_dim(table, start, held, 0)
            for table in (pick_all, first_all, second_all, sign_all)
        )
        hidden = jnp.where(section_pos == 0, entry, arriving)
        hidden = barrier(hidden)
        wide = hidden.astype(jnp.float32)
        inv_rms = lax.rsqrt(jnp.mean(wide * wide, axis=-1, keepdims=True) + EPSILON)
        normed = barrier((wide * inv_rms * gain_row).astype(jnp.bfloat16))
        sent = lax.dot_general(
            pick, normed, (((0,), (0,)), ((), ())), preferred_element_type=jnp.float32
        ).astype(jnp.bfloat16)
        if tick == 0:
            sent, first_all, second_all, sign_all, total, dues, starts, entries = barrier(
                (sent, first_all, second_all, sign_all, total, dues, starts, entries)
            )
        own = exchange(sent, SLICES, SHARERS)
        other = lax.ppermute(own, "expert", CORES)
        own_units = hidden_units(own)
        other_out = lax.ppermute(project(hidden_units(other)), "expert", CORES)
        own_out = project(own_units)
        both = (own_out.astype(jnp.float32) + other_out.astype(jnp.float32)).astype(jnp.bfloat16)
        logits = jnp.dot(normed, router_mat, preferred_element_type=jnp.float32)
        share = jax.nn.sigmoid(jnp.sum(logits * sign, axis=-1, keepdims=True))
        both, share, rest_share = barrier((both, share, 1.0 - share))
        parts = exchange(both, SLICES, SHARERS)
        outs = exchange(choose(total, parts).astype(jnp.bfloat16), EXPERTS, E)
        first_out, second_out = choose(first_place, outs), choose(second_place, outs)
        result = (wide + share * first_out + rest_share * second_out).astype(jnp.bfloat16)
        result, entering, due = barrier((result, entering, due))
        if tick + 1 < ticks:
            arriving = lax.ppermute(
                result, "section", [(i, i + 1) for i in range(sections - 1)]
            )
        if tick + 1 < pairs:
            entry = choose(entries[tick + 1], entering).astype(jnp.bfloat16)
        target = (due * PAIR + spot_micro) * 4 + spot_token
        held_now = (spot_block == expert) & (due >= 0) & (due < pairs)
        target = jnp.where(held_now, target, -1)
        keep = target[None, :] == jnp.arange(16, dtype=jnp.int32)[:, None]
        stored = stored + choose(keep.astype(jnp.bfloat16), result)
        if tick + 1 < ticks:
            arriving, stored, entry = barrier((arriving, stored, entry))
    stored = stored.astype(jnp.bfloat16).reshape(1, micro_count, 4, width)
    return stored[:, :, :tokens]


def solution(mesh):
    placed = (
        P(None, "expert", None),
        P("section", None, None, None),
        P("section", None),
        P("section", None, None),
        P("section", None, "expert"),
        P("section", None, "expert"),
        P("section", "expert", None),
    )
    return jax.shard_map(
        on_device,
        mesh=mesh,
        in_specs=placed,
        out_specs=P("section", None, "expert", None),
        check_vma=False,
    )
```

```python
import jax
import jax.numpy as jnp
from jax import lax
from jax.sharding import PartitionSpec as P

E = 4
MOST = 2
PAIR = 2
SHARERS = 8
EPSILON = 1e-05

SLICES = [[e * 16 + j * 2 + c for j in range(8)] for e in range(E) for c in range(2)]
EXPERTS = [[e * 16 + r for e in range(E)] for r in range(16)]
CORES = [(i, i ^ 1) for i in range(64)]


def exchange(block, groups, count):
    rows = block.shape[0] // count
    chunks = block.reshape(count, rows, block.shape[1])
    moved = lax.all_to_all(
        chunks, "expert", split_axis=0, concat_axis=0, axis_index_groups=groups, tiled=True
    )
    return moved.reshape(block.shape)


def choose(picks, rows):
    return jnp.dot(picks, rows, preferred_element_type=jnp.float32)


def tables(route_all, expert, rest, tokens):
    micro_count, requests, _ = route_all.shape
    rows = PAIR * E * MOST
    spots = micro_count * E * tokens

    def column(values):
        return values[:, None]

    spot = jnp.arange(spots, dtype=jnp.int32)
    micro, block, token = spot // (E * tokens), spot // tokens % E, spot % tokens
    seat = (block * (requests // E // tokens) + rest) * tokens + token
    seats = column(seat) == jnp.arange(requests, dtype=jnp.int32)[None, :]
    listed = jnp.transpose(route_all, (0, 2, 1)).reshape(2 * micro_count, requests)
    named = lax.dot_general(
        seats.astype(jnp.bfloat16),
        listed.astype(jnp.bfloat16),
        (((1,), (1,)), ((), ())),
        preferred_element_type=jnp.float32,
    )
    at = jnp.arange(2 * micro_count, dtype=jnp.int32)[None, :]
    first = jnp.sum(jnp.where(at == 2 * column(micro), named, 0.0), axis=1, keepdims=True)
    second = jnp.sum(jnp.where(at == 2 * column(micro) + 1, named, 0.0), axis=1, keepdims=True)
    first, second = lax.optimization_barrier((first, second))
    first, second = first.astype(jnp.int32), second.astype(jnp.int32)
    group = spot // tokens
    earlier = (column(group) == group[None, :]) & (column(spot) > spot[None, :])
    earlier = earlier.astype(jnp.bfloat16)
    begin = column(group % (PAIR * E)) * MOST

    def slots(hits, lanes):
        before = jnp.dot(earlier, hits.astype(jnp.bfloat16), preferred_element_type=jnp.float32)
        return before.astype(jnp.int32) == lanes[None, :] % rows - begin

    lanes = jnp.arange(SHARERS * rows, dtype=jnp.int32)
    hits = jnp.broadcast_to((first == expert) | (second == expert), (spots, SHARERS * rows))
    pick = (hits & slots(hits, lanes)).astype(jnp.bfloat16)
    lanes = jnp.arange(E * rows, dtype=jnp.int32)
    first_hit = first == lanes[None, :] // rows
    second_hit = second == lanes[None, :] // rows
    fits = slots(first_hit | second_hit, lanes)
    place = [(hit & fits).astype(jnp.bfloat16) for hit in (first_hit, second_hit)]
    ids = jnp.arange(E, dtype=jnp.int32)[None, :]
    sign = (first == ids).astype(jnp.float32) - (second == ids).astype(jnp.float32)
    return lax.optimization_barrier((pick, place[0], place[1], sign))


def on_device(inputs, routes, norm_gain, router, w_gate, w_up, w_down):
    barrier = lax.optimization_barrier
    sections = lax.axis_size("section")
    section_pos = lax.axis_index("section")
    member_pos = lax.axis_index("expert")
    expert, rest = member_pos // 16, member_pos % 16
    micro_count, tokens, width = inputs.shape
    pairs = micro_count // PAIR
    held = PAIR * E * tokens
    sent_rows = PAIR * E * MOST
    ticks = pairs + sections - 1
    gain_row, router_mat = norm_gain[0], router[0]
    gate_mat, up_mat, down_mat = w_gate[0], w_up[0], w_down[0]

    def hidden_units(rows):
        gate_value = jnp.dot(rows, gate_mat, preferred_element_type=jnp.float32)
        up_value = jnp.dot(rows, up_mat, preferred_element_type=jnp.float32)
        gate_value, up_value = barrier((gate_value, up_value))
        return barrier((jax.nn.silu(gate_value) * up_value).astype(jnp.bfloat16))

    def project(units):
        return barrier(
            jnp.dot(units, down_mat, preferred_element_type=jnp.float32).astype(jnp.bfloat16)
        )

    pick_all, first_all, second_all, sign_all = tables(routes[0], expert, rest, tokens)

    spare = tokens * micro_count
    copies = jnp.broadcast_to(jnp.swapaxes(inputs, 0, 1)[None], (E, tokens, micro_count, width))
    entering = lax.all_to_all(
        copies, "expert", split_axis=0, concat_axis=0, axis_index_groups=EXPERTS, tiled=True
    ).reshape(E * spare, width)
    spot = jnp.arange(held, dtype=jnp.int32)
    spot_micro, spot_block, spot_token = (
        spot // (E * tokens),
        spot // tokens % E,
        spot % tokens,
    )

    def entry_picks(pair):
        source = spot_block * spare + spot_token * micro_count + pair * PAIR + spot_micro
        picks = source[:, None] == jnp.arange(E * spare, dtype=jnp.int32)[None, :]
        return picks.astype(jnp.bfloat16)

    total = jnp.arange(E * sent_rows, dtype=jnp.int32)[:, None] % sent_rows
    total = total == jnp.arange(SHARERS * sent_rows, dtype=jnp.int32)[None, :] % sent_rows
    total = total.astype(jnp.bfloat16)

    dues = [jnp.int32(tick) - section_pos for tick in range(ticks)]
    starts = [(jnp.clip(due, 0, pairs - 1) * held).astype(jnp.uint32) for due in dues]
    few = 2 * PAIR * MOST
    lane = jnp.arange(few, dtype=jnp.int32)
    lane_row = jnp.where(lane < PAIR * MOST, lane // MOST * (E * MOST) + lane % MOST, -E * MOST)
    experts = jnp.arange(E, dtype=jnp.int32)[:, None]
    few_rows = (lane_row[None, :] + experts * MOST).reshape(E * few)
    few_total = few_rows[:, None] == jnp.arange(SHARERS * sent_rows, dtype=jnp.int32)[None, :] % sent_rows
    few_total = few_total.astype(jnp.bfloat16)
    few_at = jnp.where(lane_row >= 0, lane_row + expert * MOST, -E * sent_rows)
    few_at = (few_at[None, :] + experts * sent_rows).reshape(E * few)
    few_columns = jnp.arange(E * sent_rows, dtype=jnp.int32)[:, None] == few_at[None, :]
    seat = jnp.arange(4 * PAIR, dtype=jnp.int32)
    seat_spot = jnp.where(seat % 4 < tokens, (seat // 4 * E + expert) * tokens + seat % 4, -1)
    own_seats = (seat_spot[:, None] == spot[None, :]).astype(jnp.bfloat16)

    def few_place(table):
        part = lax.dynamic_slice_in_dim(table, starts[-1], held, 0)
        part = choose(own_seats, part).astype(jnp.bfloat16)
        return choose(part, few_columns.astype(jnp.bfloat16)).astype(jnp.bfloat16)

    last = (few_total, own_seats, few_place(first_all), few_place(second_all))
    entries = [entry_picks(pair) for pair in range(pairs)]
    entry = choose(entries[0], entering).astype(jnp.bfloat16)
    arriving = jnp.zeros((held, width), jnp.bfloat16)
    stored = jnp.zeros((16, width), jnp.float32)
    for tick in range(ticks):
        due, start = dues[tick], starts[tick]
        pick, first_place, second_place, sign = (
            lax.dynamic_slice_in_dim(table, start, held, 0)
            for table in (pick_all, first_all, second_all, sign_all)
        )
        hidden = jnp.where(section_pos == 0, entry, arriving)
        hidden = barrier(hidden)
        wide = hidden.astype(jnp.float32)
        inv_rms = lax.rsqrt(jnp.mean(wide * wide, axis=-1, keepdims=True) + EPSILON)
        normed = barrier((wide * inv_rms * gain_row).astype(jnp.bfloat16))
        sent = lax.dot_general(
            pick, normed, (((0,), (0,)), ((), ())), preferred_element_type=jnp.float32
        ).astype(jnp.bfloat16)
        if tick == 0:
            sent, first_all, second_all, sign_all, total, dues, starts, entries, last = barrier(
                (sent, first_all, second_all, sign_all, total, dues, starts, entries, last)
            )
        own = exchange(sent, SLICES, SHARERS)
        if tick + 1 == ticks:
            own, normed, hidden, share_seats = barrier((own, normed, hidden, last[1]))
        other = lax.ppermute(own, "expert", CORES)
        own_units = hidden_units(own)
        other_out = lax.ppermute(project(hidden_units(other)), "expert", CORES)
        own_out = project(own_units)
        both = (own_out.astype(jnp.float32) + other_out.astype(jnp.float32)).astype(jnp.bfloat16)
        logits = jnp.dot(normed, router_mat, preferred_element_type=jnp.float32)
        share = jax.nn.sigmoid(jnp.sum(logits * sign, axis=-1, keepdims=True))
        if tick + 1 == ticks:
            total, own_seats, first_place, second_place = last
            wide = choose(share_seats, hidden)
            share = jnp.dot(share_seats.astype(jnp.float32), share, precision=lax.Precision.HIGHEST)
        both, share, rest_share, wide = barrier((both, share, 1.0 - share, wide))
        parts = exchange(both, SLICES, SHARERS)
        outs = exchange(choose(total, parts).astype(jnp.bfloat16), EXPERTS, E)
        first_out, second_out = choose(first_place, outs), choose(second_place, outs)
        result = (wide + share * first_out + rest_share * second_out).astype(jnp.bfloat16)
        if tick + 1 == ticks:
            result, due = barrier((result, due))
            here = jnp.arange(pairs, dtype=jnp.int32)[:, None, None] == due
            placed = jnp.where(here, result.astype(jnp.float32)[None], 0.0)
            stored = stored + placed.reshape(stored.shape)
            break
        result, entering, due = barrier((result, entering, due))
        arriving = lax.ppermute(result, "section", [(i, i + 1) for i in range(sections - 1)])
        if tick + 1 < pairs:
            entry = choose(entries[tick + 1], entering).astype(jnp.bfloat16)
        target = (due * PAIR + spot_micro) * 4 + spot_token
        held_now = (spot_block == expert) & (due >= 0) & (due < pairs)
        target = jnp.where(held_now, target, -1)
        keep = target[None, :] == jnp.arange(16, dtype=jnp.int32)[:, None]
        stored = stored + choose(keep.astype(jnp.bfloat16), result)
        arriving, stored, entry = barrier((arriving, stored, entry))
    stored = stored.astype(jnp.bfloat16).reshape(1, micro_count, 4, width)
    return stored[:, :, :tokens]


def solution(mesh):
    placed = (
        P(None, "expert", None),
        P("section", None, None, None),
        P("section", None),
        P("section", None, None),
        P("section", None, "expert"),
        P("section", None, "expert"),
        P("section", "expert", None),
    )
    return jax.shard_map(
        on_device,
        mesh=mesh,
        in_specs=placed,
        out_specs=P("section", None, "expert", None),
        check_vma=False,
    )
```

```python
import jax
import jax.numpy as jnp
from jax import lax
from jax.sharding import PartitionSpec as P

E = 4
MOST = 2
PAIR = 2
SHARERS = 8
EPSILON = 1e-05

SLICES = [[e * 16 + j * 2 + c for j in range(8)] for e in range(E) for c in range(2)]
EXPERTS = [[e * 16 + r for e in range(E)] for r in range(16)]
CORES = [(i, i ^ 1) for i in range(64)]


def exchange(block, groups, count):
    rows = block.shape[0] // count
    chunks = block.reshape(count, rows, block.shape[1])
    moved = lax.all_to_all(
        chunks, "expert", split_axis=0, concat_axis=0, axis_index_groups=groups, tiled=True
    )
    return moved.reshape(block.shape)


def choose(picks, rows):
    return jnp.dot(picks, rows, preferred_element_type=jnp.float32)


def tables(route_all, expert, rest, tokens):
    micro_count, requests, _ = route_all.shape
    rows = PAIR * E * MOST
    spots = micro_count * E * tokens

    def column(values):
        return values[:, None]

    spot = jnp.arange(spots, dtype=jnp.int32)
    micro, block, token = spot // (E * tokens), spot // tokens % E, spot % tokens
    seat = (block * (requests // E // tokens) + rest) * tokens + token
    seats = column(seat) == jnp.arange(requests, dtype=jnp.int32)[None, :]
    listed = jnp.transpose(route_all, (0, 2, 1)).reshape(2 * micro_count, requests)
    named = lax.dot_general(
        seats.astype(jnp.bfloat16),
        listed.astype(jnp.bfloat16),
        (((1,), (1,)), ((), ())),
        preferred_element_type=jnp.float32,
    )
    at = jnp.arange(2 * micro_count, dtype=jnp.int32)[None, :]
    first = jnp.sum(jnp.where(at == 2 * column(micro), named, 0.0), axis=1, keepdims=True)
    second = jnp.sum(jnp.where(at == 2 * column(micro) + 1, named, 0.0), axis=1, keepdims=True)
    first, second = lax.optimization_barrier((first, second))
    first, second = first.astype(jnp.int32), second.astype(jnp.int32)
    group = spot // tokens
    earlier = (column(group) == group[None, :]) & (column(spot) > spot[None, :])
    earlier = earlier.astype(jnp.bfloat16)
    begin = column(group % (PAIR * E)) * MOST

    def slots(hits, lanes):
        before = jnp.dot(earlier, hits.astype(jnp.bfloat16), preferred_element_type=jnp.float32)
        return before.astype(jnp.int32) == lanes[None, :] % rows - begin

    lanes = jnp.arange(SHARERS * rows, dtype=jnp.int32)
    hits = jnp.broadcast_to((first == expert) | (second == expert), (spots, SHARERS * rows))
    pick = (hits & slots(hits, lanes)).astype(jnp.bfloat16)
    lanes = jnp.arange(E * rows, dtype=jnp.int32)
    first_hit = first == lanes[None, :] // rows
    second_hit = second == lanes[None, :] // rows
    fits = slots(first_hit | second_hit, lanes)
    place = [(hit & fits).astype(jnp.bfloat16) for hit in (first_hit, second_hit)]
    ids = jnp.arange(E, dtype=jnp.int32)[None, :]
    sign = (first == ids).astype(jnp.float32) - (second == ids).astype(jnp.float32)
    return lax.optimization_barrier((pick, place[0], place[1], sign))


def on_device(inputs, routes, norm_gain, router, w_gate, w_up, w_down):
    barrier = lax.optimization_barrier
    sections = lax.axis_size("section")
    section_pos = lax.axis_index("section")
    member_pos = lax.axis_index("expert")
    expert, rest = member_pos // 16, member_pos % 16
    micro_count, tokens, width = inputs.shape
    pairs = micro_count // PAIR
    held = PAIR * E * tokens
    sent_rows = PAIR * E * MOST
    ticks = pairs + sections - 1
    gain_row, router_mat = norm_gain[0], router[0]
    gate_mat, up_mat, down_mat = w_gate[0], w_up[0], w_down[0]

    def hidden_units(rows):
        gate_value = jnp.dot(rows, gate_mat, preferred_element_type=jnp.float32)
        up_value = jnp.dot(rows, up_mat, preferred_element_type=jnp.float32)
        gate_value, up_value = barrier((gate_value, up_value))
        return barrier((jax.nn.silu(gate_value) * up_value).astype(jnp.bfloat16))

    def project(units):
        return barrier(
            jnp.dot(units, down_mat, preferred_element_type=jnp.float32).astype(jnp.bfloat16)
        )

    pick_all, first_all, second_all, sign_all = tables(routes[0], expert, rest, tokens)

    spare = tokens * micro_count
    copies = jnp.broadcast_to(jnp.swapaxes(inputs, 0, 1)[None], (E, tokens, micro_count, width))
    entering = lax.all_to_all(
        copies, "expert", split_axis=0, concat_axis=0, axis_index_groups=EXPERTS, tiled=True
    ).reshape(E * spare, width)
    spot = jnp.arange(held, dtype=jnp.int32)
    spot_micro, spot_block, spot_token = (
        spot // (E * tokens),
        spot // tokens % E,
        spot % tokens,
    )

    def entry_picks(pair):
        source = spot_block * spare + spot_token * micro_count + pair * PAIR + spot_micro
        picks = source[:, None] == jnp.arange(E * spare, dtype=jnp.int32)[None, :]
        return picks.astype(jnp.bfloat16)

    total = jnp.arange(E * sent_rows, dtype=jnp.int32)[:, None] % sent_rows
    total = total == jnp.arange(SHARERS * sent_rows, dtype=jnp.int32)[None, :] % sent_rows
    total = total.astype(jnp.bfloat16)

    starts = [
        (jnp.clip(tick - section_pos, 0, pairs - 1) * held).astype(jnp.uint32)
        for tick in range(ticks)
    ]
    few = 2 * PAIR * MOST
    lane = jnp.arange(few, dtype=jnp.int32)
    lane_row = jnp.where(lane < PAIR * MOST, lane // MOST * (E * MOST) + lane % MOST, -E * MOST)
    experts = jnp.arange(E, dtype=jnp.int32)[:, None]
    few_rows = (lane_row[None, :] + experts * MOST).reshape(E * few)
    few_total = few_rows[:, None] == jnp.arange(SHARERS * sent_rows, dtype=jnp.int32)[None, :] % sent_rows
    few_total = few_total.astype(jnp.bfloat16)
    few_at = jnp.where(lane_row >= 0, lane_row + expert * MOST, -E * sent_rows)
    few_at = (few_at[None, :] + experts * sent_rows).reshape(E * few)
    few_columns = jnp.arange(E * sent_rows, dtype=jnp.int32)[:, None] == few_at[None, :]
    seat = jnp.arange(4 * PAIR, dtype=jnp.int32)
    seat_spot = (seat % PAIR * E + expert) * tokens + seat // PAIR
    seat_spot = jnp.where(seat // PAIR < tokens, seat_spot, -1)
    own_seats = (seat_spot[:, None] == spot[None, :]).astype(jnp.bfloat16)

    def few_place(table):
        part = lax.dynamic_slice_in_dim(table, starts[-1], held, 0)
        part = choose(own_seats, part).astype(jnp.bfloat16)
        return choose(part, few_columns.astype(jnp.bfloat16)).astype(jnp.bfloat16)

    line = jnp.arange(16, dtype=jnp.int32)[:, None]
    seen = jnp.arange((ticks - 1) * held, dtype=jnp.int32)
    due, spot_of = seen // held - section_pos, seen % held
    target = spot_of % tokens * micro_count + due * PAIR + spot_of // (E * tokens)
    mine = (spot_of // tokens % E == expert) & (due >= 0) & (due < pairs)
    keep_all = (jnp.where(mine, target, -1)[None, :] == line).astype(jnp.bfloat16)
    due = jnp.full((4 * PAIR,), ticks - 1, jnp.int32) - section_pos
    target = seat // PAIR * micro_count + due * PAIR + seat % PAIR
    keep_last = jnp.where((due >= 0) & (due < pairs), target, -1)
    keep_last = (keep_last[None, :] == line).astype(jnp.bfloat16)
    last = (few_total, own_seats, few_place(first_all), few_place(second_all), keep_all, keep_last)
    entries = [entry_picks(pair) for pair in range(pairs)]
    entry = choose(entries[0], entering).astype(jnp.bfloat16)
    arriving = jnp.zeros((held, width), jnp.bfloat16)
    stored, results = jnp.zeros((), jnp.float32), []
    for tick in range(ticks):
        start = starts[tick]
        pick, first_place, second_place, sign = (
            lax.dynamic_slice_in_dim(table, start, held, 0)
            for table in (pick_all, first_all, second_all, sign_all)
        )
        hidden = jnp.where(section_pos == 0, entry, arriving)
        hidden = barrier(hidden)
        wide = hidden.astype(jnp.float32)
        inv_rms = lax.rsqrt(jnp.mean(wide * wide, axis=-1, keepdims=True) + EPSILON)
        normed = barrier((wide * inv_rms * gain_row).astype(jnp.bfloat16))
        sent = lax.dot_general(
            pick, normed, (((0,), (0,)), ((), ())), preferred_element_type=jnp.float32
        ).astype(jnp.bfloat16)
        if tick == 0:
            sent, first_all, second_all, sign_all, total, starts, entries, last = barrier(
                (sent, first_all, second_all, sign_all, total, starts, entries, last)
            )
        own = exchange(sent, SLICES, SHARERS)
        if tick + 1 == ticks:
            own, normed, hidden, share_seats, results = barrier(
                (own, normed, hidden, last[1], results)
            )
        other = lax.ppermute(own, "expert", CORES)
        own_units = hidden_units(own)
        other_out = lax.ppermute(project(hidden_units(other)), "expert", CORES)
        own_out = project(own_units)
        both = (own_out.astype(jnp.float32) + other_out.astype(jnp.float32)).astype(jnp.bfloat16)
        logits = jnp.dot(normed, router_mat, preferred_element_type=jnp.float32)
        share = jax.nn.sigmoid(jnp.sum(logits * sign, axis=-1, keepdims=True))
        if tick + 1 == ticks:
            total, own_seats, first_place, second_place, keep_all, keep_last = last
            stored = choose(keep_all, jnp.concatenate(results, axis=0))
            wide = choose(share_seats, hidden)
            share = jnp.dot(share_seats.astype(jnp.float32), share, precision=lax.Precision.HIGHEST)
        both, share, rest_share, wide, stored = barrier((both, share, 1.0 - share, wide, stored))
        parts = exchange(both, SLICES, SHARERS)
        outs = exchange(choose(total, parts).astype(jnp.bfloat16), EXPERTS, E)
        first_out, second_out = choose(first_place, outs), choose(second_place, outs)
        result = (wide + share * first_out + rest_share * second_out).astype(jnp.bfloat16)
        if tick + 1 == ticks:
            stored = stored + choose(keep_last, result)
            break
        result, entering = barrier((result, entering))
        results.append(result)
        arriving = lax.ppermute(result, "section", [(i, i + 1) for i in range(sections - 1)])
        if tick + 1 < pairs:
            entry = choose(entries[tick + 1], entering).astype(jnp.bfloat16)
        arriving, entry = barrier((arriving, entry))
    stored = stored.astype(jnp.bfloat16)[: tokens * micro_count]
    return jnp.swapaxes(stored.reshape(1, tokens, micro_count, width), 1, 2)


def solution(mesh):
    placed = (
        P(None, "expert", None),
        P("section", None, None, None),
        P("section", None),
        P("section", None, None),
        P("section", None, "expert"),
        P("section", None, "expert"),
        P("section", "expert", None),
    )
    return jax.shard_map(
        on_device,
        mesh=mesh,
        in_specs=placed,
        out_specs=P("section", None, "expert", None),
        check_vma=False,
    )
```

```python
import jax
import jax.numpy as jnp
from jax import lax
from jax.sharding import PartitionSpec as P

E = 4
MOST = 2
PAIR = 2
SHARERS = 8
EPSILON = 1e-05

SLICES = [[e * 16 + j * 2 + c for j in range(8)] for e in range(E) for c in range(2)]
EXPERTS = [[e * 16 + r for e in range(E)] for r in range(16)]
CORES = [(i, i ^ 1) for i in range(64)]


def exchange(block, groups, count):
    rows = block.shape[0] // count
    chunks = block.reshape(count, rows, block.shape[1])
    moved = lax.all_to_all(
        chunks, "expert", split_axis=0, concat_axis=0, axis_index_groups=groups, tiled=True
    )
    return moved.reshape(block.shape)


def choose(picks, rows):
    return jnp.dot(picks, rows, preferred_element_type=jnp.float32)


def tables(route_all, expert, rest, tokens):
    micro_count, requests, _ = route_all.shape
    rows = PAIR * E * MOST
    spots = micro_count * E * tokens

    def column(values):
        return values[:, None]

    spot = jnp.arange(spots, dtype=jnp.int32)
    micro, block, token = spot // (E * tokens), spot // tokens % E, spot % tokens
    seat = (block * (requests // E // tokens) + rest) * tokens + token
    seats = column(seat) == jnp.arange(requests, dtype=jnp.int32)[None, :]
    listed = jnp.transpose(route_all, (0, 2, 1)).reshape(2 * micro_count, requests)
    named = lax.dot_general(
        seats.astype(jnp.bfloat16),
        listed.astype(jnp.bfloat16),
        (((1,), (1,)), ((), ())),
        preferred_element_type=jnp.float32,
    )
    at = jnp.arange(2 * micro_count, dtype=jnp.int32)[None, :]
    first = jnp.sum(jnp.where(at == 2 * column(micro), named, 0.0), axis=1, keepdims=True)
    second = jnp.sum(jnp.where(at == 2 * column(micro) + 1, named, 0.0), axis=1, keepdims=True)
    first, second = lax.optimization_barrier((first, second))
    first, second = first.astype(jnp.int32), second.astype(jnp.int32)
    group = spot // tokens
    earlier = (column(group) == group[None, :]) & (column(spot) > spot[None, :])
    earlier = earlier.astype(jnp.bfloat16)
    begin = column(group % (PAIR * E)) * MOST

    def slots(hits, lanes):
        before = jnp.dot(earlier, hits.astype(jnp.bfloat16), preferred_element_type=jnp.float32)
        return before.astype(jnp.int32) == lanes[None, :] % rows - begin

    lanes = jnp.arange(SHARERS * rows, dtype=jnp.int32)
    hits = jnp.broadcast_to((first == expert) | (second == expert), (spots, SHARERS * rows))
    pick = (hits & slots(hits, lanes)).astype(jnp.bfloat16)
    lanes = jnp.arange(E * rows, dtype=jnp.int32)
    first_hit = first == lanes[None, :] // rows
    second_hit = second == lanes[None, :] // rows
    fits = slots(first_hit | second_hit, lanes)
    place = [(hit & fits).astype(jnp.bfloat16) for hit in (first_hit, second_hit)]
    ids = jnp.arange(E, dtype=jnp.int32)[None, :]
    sign = (first == ids).astype(jnp.float32) - (second == ids).astype(jnp.float32)
    return lax.optimization_barrier((pick, place[0], place[1], sign))


def on_device(inputs, routes, norm_gain, router, w_gate, w_up, w_down):
    barrier = lax.optimization_barrier
    sections = lax.axis_size("section")
    section_pos = lax.axis_index("section")
    member_pos = lax.axis_index("expert")
    expert, rest = member_pos // 16, member_pos % 16
    micro_count, tokens, width = inputs.shape
    pairs = micro_count // PAIR
    held = PAIR * E * tokens
    sent_rows = PAIR * E * MOST
    ticks = pairs + sections - 1
    gain_row, router_mat = norm_gain[0], router[0]
    gate_mat, up_mat, down_mat = w_gate[0], w_up[0], w_down[0]

    def hidden_units(rows):
        gate_value = jnp.dot(rows, gate_mat, preferred_element_type=jnp.float32)
        up_value = jnp.dot(rows, up_mat, preferred_element_type=jnp.float32)
        gate_value, up_value = barrier((gate_value, up_value))
        return barrier((jax.nn.silu(gate_value) * up_value).astype(jnp.bfloat16))

    def project(units):
        return barrier(
            jnp.dot(units, down_mat, preferred_element_type=jnp.float32).astype(jnp.bfloat16)
        )

    pick_all, first_all, second_all, sign_all = tables(routes[0], expert, rest, tokens)

    spare = tokens * micro_count
    spot = jnp.arange(held, dtype=jnp.int32)
    spot_micro, spot_block, spot_token = (
        spot // (E * tokens),
        spot // tokens % E,
        spot % tokens,
    )

    def entry_picks(pair):
        source = spot_block * spare + spot_token * micro_count + pair * PAIR + spot_micro
        picks = source[:, None] == jnp.arange(E * spare, dtype=jnp.int32)[None, :]
        return picks.astype(jnp.bfloat16)

    total = jnp.arange(E * sent_rows, dtype=jnp.int32)[:, None] % sent_rows
    total = total == jnp.arange(SHARERS * sent_rows, dtype=jnp.int32)[None, :] % sent_rows
    total = total.astype(jnp.bfloat16)

    starts = [
        (jnp.clip(tick - section_pos, 0, pairs - 1) * held).astype(jnp.uint32)
        for tick in range(ticks)
    ]
    few = 2 * PAIR * MOST
    lane = jnp.arange(few, dtype=jnp.int32)
    lane_row = jnp.where(lane < PAIR * MOST, lane // MOST * (E * MOST) + lane % MOST, -E * MOST)
    experts = jnp.arange(E, dtype=jnp.int32)[:, None]
    few_rows = (lane_row[None, :] + experts * MOST).reshape(E * few)
    few_total = few_rows[:, None] == jnp.arange(SHARERS * sent_rows, dtype=jnp.int32)[None, :] % sent_rows
    few_total = few_total.astype(jnp.bfloat16)
    few_at = jnp.where(lane_row >= 0, lane_row + expert * MOST, -E * sent_rows)
    few_at = (few_at[None, :] + experts * sent_rows).reshape(E * few)
    few_columns = jnp.arange(E * sent_rows, dtype=jnp.int32)[:, None] == few_at[None, :]
    seat = jnp.arange(4 * PAIR, dtype=jnp.int32)
    seat_spot = (seat % PAIR * E + expert) * tokens + seat // PAIR
    seat_spot = jnp.where(seat // PAIR < tokens, seat_spot, -1)
    own_seats = (seat_spot[:, None] == spot[None, :]).astype(jnp.bfloat16)

    def few_place(table):
        part = lax.dynamic_slice_in_dim(table, starts[-1], held, 0)
        part = choose(own_seats, part).astype(jnp.bfloat16)
        return choose(part, few_columns.astype(jnp.bfloat16)).astype(jnp.bfloat16)

    line = jnp.arange(16, dtype=jnp.int32)[:, None]
    seen = jnp.arange((ticks - 1) * held, dtype=jnp.int32)
    due, spot_of = seen // held - section_pos, seen % held
    target = spot_of % tokens * micro_count + due * PAIR + spot_of // (E * tokens)
    mine = (spot_of // tokens % E == expert) & (due >= 0) & (due < pairs)
    keep_all = (jnp.where(mine, target, -1)[None, :] == line).astype(jnp.bfloat16)
    due = jnp.full((4 * PAIR,), ticks - 1, jnp.int32) - section_pos
    target = seat // PAIR * micro_count + due * PAIR + seat % PAIR
    keep_last = jnp.where((due >= 0) & (due < pairs), target, -1)
    keep_last = (keep_last[None, :] == line).astype(jnp.bfloat16)
    last = (few_total, own_seats, few_place(first_all), few_place(second_all), keep_all, keep_last)
    entries = [entry_picks(pair) for pair in range(pairs)]
    own_rows, at_entry = jnp.swapaxes(inputs, 0, 1), section_pos == 0
    (own_rows, at_entry, pick_all, first_all, second_all, sign_all, total, starts, entries, last) = barrier(
        (own_rows, at_entry, pick_all, first_all, second_all, sign_all, total, starts, entries, last)
    )
    copies = jnp.broadcast_to(own_rows[None], (E, tokens, micro_count, width))
    entering = lax.all_to_all(
        copies, "expert", split_axis=0, concat_axis=0, axis_index_groups=EXPERTS, tiled=True
    ).reshape(E * spare, width)
    entry = choose(entries[0], entering).astype(jnp.bfloat16)
    arriving = jnp.zeros((held, width), jnp.bfloat16)
    stored, results = jnp.zeros((), jnp.float32), []
    for tick in range(ticks):
        start = starts[tick]
        pick, first_place, second_place, sign = (
            lax.dynamic_slice_in_dim(table, start, held, 0)
            for table in (pick_all, first_all, second_all, sign_all)
        )
        hidden = jnp.where(at_entry, entry, arriving)
        hidden = barrier(hidden)
        wide = hidden.astype(jnp.float32)
        inv_rms = lax.rsqrt(jnp.mean(wide * wide, axis=-1, keepdims=True) + EPSILON)
        normed = barrier((wide * inv_rms * gain_row).astype(jnp.bfloat16))
        sent = lax.dot_general(
            pick, normed, (((0,), (0,)), ((), ())), preferred_element_type=jnp.float32
        ).astype(jnp.bfloat16)
        if tick == 0:
            sent, first_all, second_all, sign_all, total, starts, entries, last = barrier(
                (sent, first_all, second_all, sign_all, total, starts, entries, last)
            )
        own = exchange(sent, SLICES, SHARERS)
        if tick + 1 == ticks:
            own, normed, hidden, share_seats, results = barrier(
                (own, normed, hidden, last[1], results)
            )
        other = lax.ppermute(own, "expert", CORES)
        own_units = hidden_units(own)
        other_out = lax.ppermute(project(hidden_units(other)), "expert", CORES)
        own_out = project(own_units)
        both = (own_out.astype(jnp.float32) + other_out.astype(jnp.float32)).astype(jnp.bfloat16)
        logits = jnp.dot(normed, router_mat, preferred_element_type=jnp.float32)
        share = jax.nn.sigmoid(jnp.sum(logits * sign, axis=-1, keepdims=True))
        if tick + 1 == ticks:
            total, own_seats, first_place, second_place, keep_all, keep_last = last
            stored = choose(keep_all, jnp.concatenate(results, axis=0))
            wide = choose(share_seats, hidden)
            share = jnp.dot(share_seats.astype(jnp.float32), share, precision=lax.Precision.HIGHEST)
        both, share, rest_share, wide, stored = barrier((both, share, 1.0 - share, wide, stored))
        parts = exchange(both, SLICES, SHARERS)
        outs = exchange(choose(total, parts).astype(jnp.bfloat16), EXPERTS, E)
        first_out, second_out = choose(first_place, outs), choose(second_place, outs)
        result = (wide + share * first_out + rest_share * second_out).astype(jnp.bfloat16)
        if tick + 1 == ticks:
            stored = stored + choose(keep_last, result)
            break
        result, entering = barrier((result, entering))
        results.append(result)
        arriving = lax.ppermute(result, "section", [(i, i + 1) for i in range(sections - 1)])
        if tick + 1 < pairs:
            entry = choose(entries[tick + 1], entering).astype(jnp.bfloat16)
        arriving, entry = barrier((arriving, entry))
    stored = stored.astype(jnp.bfloat16)[: tokens * micro_count]
    return jnp.swapaxes(stored.reshape(1, tokens, micro_count, width), 1, 2)


def solution(mesh):
    placed = (
        P(None, "expert", None),
        P("section", None, None, None),
        P("section", None),
        P("section", None, None),
        P("section", None, "expert"),
        P("section", None, "expert"),
        P("section", "expert", None),
    )
    return jax.shard_map(
        on_device,
        mesh=mesh,
        in_specs=placed,
        out_specs=P("section", None, "expert", None),
        check_vma=False,
    )
```
